32 devices in a mesh: freq: 2 (over x), clus: 8 (over z, y), rhs: 2 (over core).
Axes of the slice: x: 2, y: 2, z: 4, core: 2. Of those that a mesh axis runs over, the one named last changes fastest.
Arguments:
- input_columns: bfloat16 [256, 2, 128, 128], P(('freq', 'clus'), None, 'rhs'), parts along dimension 0, may hold values from -6 to 6
- near_blocks: bfloat16 [256, 7, 2, 128, 128], P(('freq', 'clus')), parts along dimension 0, may hold values from -0.125 to 0.125
- near_off: int32 [128, 7], P('clus'), may hold values from -16 to 16, as said below
- basis_in: bfloat16 [256, 2, 128, 64], P(('freq', 'clus')), parts along dimension 0, may hold values from -0.375 to 0.375
- coupling: bfloat16 [16, 8, 4, 2, 64, 64], P(('freq', 'clus')), parts along dimension 0, may hold values from -0.375 to 0.375
- basis_out: bfloat16 [256, 2, 64, 128], P(('freq', 'clus')), parts along dimension 0, may hold values from -0.5 to 0.5
- far_pairs: int32 [8, 8, 4, 2], replicated, may hold values from 0 to 15
- far_rank: int32 [8, 8, 4], replicated, may hold values from 0 to 64, as said below
Outputs:
- first_image: bfloat16 [256, 2, 128, 128], P(('freq', 'clus'), None, 'rhs'), parts along dimension 0
- second_image: bfloat16 [256, 2, 128, 128], P(('freq', 'clus'), None, 'rhs'), parts along dimension 0
The draws below stay inside these ranges and needn't reach their ends.
There are 2 independent parts, one for each index of `freq`. The reference program is written for one: setup_inputs(seed, part) draws one part's arguments, and reference() takes and returns one part's arrays. A program takes and returns all parts, laid end to end along the dimension named above; an argument that names none is the same for every part. Nothing has to cross between parts.
Inputs may be any that keep to these rules, and one draw needn't show every extreme that they name: `near_off`: each row holds 7 distinct offsets, the first of them 0. `far_rank`: a rank of 0 marks an empty slot.
All inputs are finite; a program needn't handle non-finite values.
Results may differ from the reference program's by a relative error of at most 0.0056.
Values may be sent and summed in bfloat16 or wider, within the bound.
A program may use at most 128 MiB of HBM per device.

```python
import jax
import jax.numpy as jnp
from jax import lax

CL = 128
RANK = 64
NEAR_PER = 7
CAP = 4
C_DEV = 16
CLUSTERS = 128
RHS = 128
N_CLUS = 8


def draw_near_off(key, part):
    row_keys = jax.random.split(jax.random.fold_in(key, 11), CLUSTERS)
    shuffled = jax.vmap(lambda row_key: jax.random.permutation(row_key, 2 * C_DEV))(row_keys).astype(jnp.int32)
    offsets = jnp.where(shuffled < C_DEV, shuffled - C_DEV, shuffled - C_DEV + 1).astype(jnp.int32)
    first_row = offsets[0]
    scores = jnp.where(first_row == -C_DEV, -2, jnp.where(first_row == C_DEV, -1, jnp.arange(2 * C_DEV, dtype=jnp.int32)))
    first_row = first_row[jnp.argsort(scores, stable=True)]
    offsets = offsets.at[0].set(first_row)
    picks = offsets[:, :NEAR_PER - 1]
    return jnp.concatenate([jnp.zeros((CLUSTERS, 1), jnp.int32), picks], 1).astype(jnp.int32)


def draw_far_pairs(key, part):
    values = jax.random.randint(jax.random.fold_in(key, 23), (N_CLUS, N_CLUS, CAP, 2), 0, C_DEV).astype(jnp.int32)
    values = values.at[0, 0, 0, 0].set(0)
    values = values.at[0, 0, 0, 1].set(C_DEV - 1)
    return values


def draw_far_rank(key, part):
    pair_level = jax.random.randint(jax.random.fold_in(key, 31), (N_CLUS, N_CLUS, 1), 2, 10)
    trial = jax.random.randint(jax.random.fold_in(key, 37), (N_CLUS, N_CLUS, CAP), 0, 10)
    ranks = jax.random.randint(jax.random.fold_in(key, 41), (N_CLUS, N_CLUS, CAP), RANK // 4, RANK + 1)
    ranks = jnp.where(trial < pair_level, ranks, 0).astype(jnp.int32)
    ranks = ranks.at[0, 0, 0].set(RANK)
    ranks = ranks.at[0, 0, 1].set(0)
    return ranks


def level_of(own_key, extent, cuts, low, high):
    def one(position, shards_of):
        draws = jax.random.uniform(jax.random.fold_in(jax.random.fold_in(own_key, 6), position), (shards_of,), jnp.float32, low / len(cuts), high / len(cuts))
        return jnp.repeat(jnp.exp(draws), extent[position] // shards_of).reshape((-1,) + (1,) * (len(extent) - position - 1))

    loudness = one(*cuts[0])
    for cut in cuts[1:]:
        loudness = loudness * one(*cut)
    return loudness


def gaussian(key, extent, scale, bound, shards=(), kind=jnp.bfloat16):
    drawn = scale * jax.random.normal(key, extent, jnp.float32)
    if shards:
        drawn = drawn * level_of(key, extent, shards, -0.22, 0.18)
    return jnp.clip(drawn, -bound, bound).astype(kind)


def setup_inputs(seed: int = 0, part: int = 0) -> dict:
    streams_of = jax.random.split(jax.random.key(seed), 9)
    own_keys = jax.random.split(jax.random.fold_in(streams_of[8], part), 9)
    return {
        "input_columns": gaussian(own_keys[0], (CLUSTERS, 2, RHS, CL), 1.0, 6.0, ((0, 8), (2, 2))),
        "near_blocks": gaussian(own_keys[1], (CLUSTERS, NEAR_PER, 2, CL, CL), (2 * CL * NEAR_PER) ** -0.5, 0.125, ((0, 8),)),
        "near_off": draw_near_off(jax.random.fold_in(streams_of[8], 71), part),
        "basis_in": gaussian(own_keys[3], (CLUSTERS, 2, CL, RANK), (2 * CL) ** -0.5, 0.375, ((0, 8),)),
        "coupling": gaussian(own_keys[4], (N_CLUS, N_CLUS, CAP, 2, RANK, RANK), (2 * RANK * N_CLUS * CAP // C_DEV) ** -0.5, 0.375, ((0, 8),)),
        "basis_out": gaussian(own_keys[5], (CLUSTERS, 2, RANK, CL), (2 * RANK) ** -0.5, 0.5, ((0, 8),)),
        "far_pairs": draw_far_pairs(jax.random.fold_in(streams_of[8], 71), part),
        "far_rank": draw_far_rank(jax.random.fold_in(streams_of[8], 71), part),
    }


def basis_inward(basis):
    real_part = basis[:, 0]
    imag_part = basis[:, 1]
    upper = jnp.concatenate([real_part, imag_part], -1)
    lower = jnp.concatenate([-imag_part, real_part], -1)
    return jnp.stack([upper, lower], 1)


def basis_outward(basis):
    real_part = basis[:, 0]
    imag_part = basis[:, 1]
    upper = jnp.stack([real_part, imag_part], 2)
    lower = jnp.stack([-imag_part, real_part], 2)
    return jnp.concatenate([upper, lower], 1)


def coupling_square(coupling):
    real_part = coupling[..., 0, :, :]
    imag_part = coupling[..., 1, :, :]
    upper = jnp.concatenate([real_part, imag_part], -1)
    lower = jnp.concatenate([-imag_part, real_part], -1)
    return jnp.concatenate([upper, lower], -2)


def rounded(values):
    narrow = lax.optimization_barrier(values.astype(jnp.bfloat16))
    return narrow.astype(jnp.float32)


def transposed_apply(columns, near_blocks, near_off, basis_in, coupling, basis_out, far_pairs, far_rank):
    total = columns.shape[0]
    width = basis_in.shape[-1]
    highest = lax.Precision.HIGHEST
    floats = columns.astype(jnp.float32)
    neighbour = (jnp.arange(total, dtype=jnp.int32)[:, None] + near_off).astype(jnp.int32)
    inside = ((neighbour >= 0) & (neighbour < total)).astype(jnp.float32)
    gathered = floats[jnp.clip(neighbour, 0, total - 1)] * inside[:, :, None, None, None]
    products = jnp.einsum('cjprt,cjqts->cpqrs', gathered, near_blocks.astype(jnp.float32), precision=highest)
    near_real = products[:, 0, 0] - products[:, 1, 1]
    near_imag = products[:, 0, 1] + products[:, 1, 0]
    coeffs = rounded(jnp.einsum('cprt,cptk->crk', floats, basis_inward(basis_in).astype(jnp.float32), precision=highest))
    sender = jnp.arange(N_CLUS, dtype=jnp.int32)[:, None, None]
    receiver = jnp.arange(N_CLUS, dtype=jnp.int32)[None, :, None]
    source = (sender * C_DEV + far_pairs[..., 0]).astype(jnp.int32)
    target = (receiver * C_DEV + far_pairs[..., 1]).astype(jnp.int32)
    rank_mask = ((jnp.arange(2 * width, dtype=jnp.int32) % width) < far_rank[..., None]).astype(jnp.float32)
    picked = coeffs[source] * rank_mask[:, :, :, None, :]
    square = coupling_square(jnp.transpose(coupling, (1, 0, 2, 3, 4, 5))).astype(jnp.float32)
    weighted = jnp.einsum('edjrk,edjkl->edjrl', picked, square, precision=highest) * rank_mask[:, :, :, None, :]
    flat = weighted.reshape((-1,) + weighted.shape[3:])
    summed = rounded(jax.ops.segment_sum(flat, target.reshape(-1), num_segments=total))
    far_term = jnp.einsum('crk,ckqs->cqrs', summed, basis_outward(basis_out).astype(jnp.float32), precision=highest)
    return (jnp.stack([near_real, near_imag], 1) + far_term).astype(jnp.bfloat16)


def reference(input_columns, near_blocks, near_off, basis_in, coupling, basis_out, far_pairs, far_rank):
    first_image = transposed_apply(input_columns, near_blocks, near_off, basis_in, coupling, basis_out, far_pairs, far_rank)
    second_image = transposed_apply(first_image, near_blocks, near_off, basis_in, coupling, basis_out, far_pairs, far_rank)
    return (first_image, second_image)
```

```python
import functools

import jax
import jax.numpy as jnp
from jax import lax
from jax.experimental import pallas as pl
from jax.experimental.pallas import tpu as pltpu
from jax.sharding import PartitionSpec as P

F32 = jnp.float32
BF16 = jnp.bfloat16

HI_A, HI_B, LO_A, LO_B = range(4)


def complex_rows(product):
    half_rows, half_cols = product.shape[0] // 2, product.shape[1] // 2
    real = product[:half_rows, :half_cols] - product[half_rows:, half_cols:]
    imag = product[:half_rows, half_cols:] + product[half_rows:, :half_cols]
    return real, imag


def kernel(
    n, off, pairs, rank, columns, near_hbm, basis_in, coupling, basis_out,
    first, second,
    near, own_0, own_1, image, hi_a_0, hi_b_0, lo_a_0, lo_b_0, hi_a_1, hi_b_1, lo_a_1, lo_b_1, total, coeffs, outgoing, received, square, weighted,
    near_sem, halo_send, halo_recv, slot_send, slot_recv,
):
    me = lax.axis_index("clus")
    clusters, rows, leaf = columns.shape
    half = clusters // 2
    slots = coupling.shape[1]
    width = coupling.shape[3]
    near_per = near.shape[1]
    rhs = rows // 2

    def fetch():
        return pltpu.make_async_copy(near_hbm, near, near_sem)

    fetch().start()
    barrier = pltpu.get_barrier_semaphore()

    @pl.loop(1, n)
    def _(k):
        pl.semaphore_signal(barrier, inc=1, device_id={"clus": lax.rem(me + k, n)})

    own = (own_0, own_1)
    buffers = ((hi_a_0, hi_b_0, lo_a_0, lo_b_0), (hi_a_1, hi_b_1, lo_a_1, lo_b_1))
    zero = jnp.zeros((rows, leaf), BF16)
    for sweep in range(2):
        own[sweep][clusters] = zero
        for buffer in buffers[sweep]:
            buffer[half] = zero

    @pl.when(me == 0)
    def _():
        for sweep in range(2):
            for chunk in (LO_A, LO_B):
                buffers[sweep][chunk][...] = jnp.zeros_like(buffers[sweep][chunk])

    @pl.when(me == n - 1)
    def _():
        for sweep in range(2):
            for chunk in (HI_A, HI_B):
                buffers[sweep][chunk][...] = jnp.zeros_like(buffers[sweep][chunk])

    pl.semaphore_wait(barrier, n - 1)

    starts = (0, half, half, 0)

    def halo(sweep, chunk):
        to_left = chunk in (HI_A, HI_B)
        source = columns if sweep == 0 else image
        peer = lax.rem(me + (n - 1 if to_left else 1), n)
        return pltpu.make_async_remote_copy(
            src_ref=source.at[pl.ds(starts[chunk], half)],
            dst_ref=buffers[sweep][chunk].at[pl.ds(0, half)],
            send_sem=halo_send.at[sweep, chunk],
            recv_sem=halo_recv.at[sweep, chunk],
            device_id={"clus": peer},
        )

    def send_halo(sweep, chunk):
        @pl.when(me > 0 if chunk in (HI_A, HI_B) else me < n - 1)
        def _():
            halo(sweep, chunk).start()

    def halo_sent(sweep, chunk):
        @pl.when(me > 0 if chunk in (HI_A, HI_B) else me < n - 1)
        def _():
            halo(sweep, chunk).wait_send()

    def wait_halo(sweep, chunk):
        @pl.when(me < n - 1 if chunk in (HI_A, HI_B) else me > 0)
        def _():
            halo(sweep, chunk).wait_recv()

    def slot_copy(sweep, k, peer, sender):
        return pltpu.make_async_remote_copy(
            src_ref=outgoing.at[sweep, peer],
            dst_ref=received.at[sweep, sender],
            send_sem=slot_send.at[sweep, k],
            recv_sem=slot_recv.at[sweep, k],
            device_id={"clus": peer},
        )

    def make_coeffs(sweep, low, high):
        source = columns if sweep == 0 else image

        @pl.loop(low, high)
        def _(c):
            v = source[c]
            basis = basis_in[c]
            by_real = jnp.dot(v, basis[0], preferred_element_type=F32)
            by_imag = jnp.dot(v, basis[1], preferred_element_type=F32)
            real = by_real[:rhs] - by_imag[rhs:]
            imag = by_imag[:rhs] + by_real[rhs:]
            coeffs[sweep, c] = jnp.concatenate([real, imag], -1).astype(BF16)

    def send_slots(sweep):
        @pl.loop(1, n)
        def _(k):
            peer = lax.rem(me + k, n)
            for j in range(slots):
                outgoing[sweep, peer, j] = coeffs[sweep, pairs[((me * n + peer) * slots + j) * 2]]
            slot_copy(sweep, k, peer, me).start()

        for j in range(slots):
            received[sweep, me, j] = coeffs[sweep, pairs[((me * n + me) * slots + j) * 2]]

    def near_phase(sweep, pieces, low, high, start, finish=None):
        @pl.loop(low, high)
        def _(c):
            product = None
            for buffers_of, base, count in pieces:
                buffer = buffers_of[sweep]
                for j in range(start, near_per, 2):
                    group = range(j, min(j + 2, near_per))
                    left, right = [], []
                    for slot in group:
                        at = c + off[c * near_per + slot] - base
                        at = jnp.where((at >= 0) & (at < count), at, count)
                        left.append(buffer[at])
                        right.append(jnp.concatenate([near[c, slot, 0], near[c, slot, 1]], -1))
                    left = left[0] if len(left) == 1 else jnp.concatenate(left, -1)
                    right = right[0] if len(right) == 1 else jnp.concatenate(right, 0)
                    term = jnp.dot(left, right, preferred_element_type=F32)
                    product = term if product is None else product + term
            real, imag = complex_rows(product)
            if start == 0:
                total[c, :rhs] = real
                total[c, rhs:] = imag
                return
            real = total[c, :rhs] + real
            imag = total[c, rhs:] + imag
            if finish is None:
                total[c, :rhs] = real
                total[c, rhs:] = imag
                return
            for target in finish:
                target[c, :rhs] = real.astype(BF16)
                target[c, rhs:] = imag.astype(BF16)

    def far(sweep):
        @pl.loop(1, n)
        def _(k):
            sender = lax.rem(me + n - k, n)
            slot_copy(sweep, k, lax.rem(me + k, n), sender).wait_recv()

        @pl.loop(0, n)
        def _(e):
            for j in range(slots):
                weighted[e, j] = jnp.dot(received[sweep, e, j], square[e, j], preferred_element_type=F32)

        @pl.loop(0, clusters)
        def _(c):
            def add(e, value):
                for j in range(slots):
                    hit = (pairs[((e * n + me) * slots + j) * 2 + 1] == c).astype(F32)
                    value = value + weighted[e, j] * hit
                return value

            gathered = lax.fori_loop(0, n, add, jnp.zeros((rhs, 2 * width), F32)).astype(BF16)
            real, imag = basis_out[c, 0], basis_out[c, 1]
            upper = jnp.concatenate([real, imag], -1)
            lower = jnp.concatenate([-imag, real], -1)
            term = jnp.dot(gathered, jnp.concatenate([upper, lower], 0), preferred_element_type=F32)
            total[c, :rhs] = total[c, :rhs] + term[:, :leaf]
            total[c, rhs:] = total[c, rhs:] + term[:, leaf:]

    send_halo(0, HI_A)
    send_halo(0, LO_A)
    make_coeffs(0, 0, clusters)
    send_slots(0)
    send_halo(0, HI_B)
    send_halo(0, LO_B)

    own_0[:clusters] = columns[...]

    @pl.loop(0, n)
    def _(e):
        for j in range(slots):
            bound = rank[(e * n + me) * slots + j]
            real, imag = coupling[e, j, 0], coupling[e, j, 1]
            full = jnp.concatenate(
                [jnp.concatenate([real, imag], -1), jnp.concatenate([-imag, real], -1)], 0
            )
            here = lax.broadcasted_iota(jnp.int32, full.shape, 0) % width
            there = lax.broadcasted_iota(jnp.int32, full.shape, 1) % width
            keep = (here < bound) & (there < bound)
            square[e, j] = jnp.where(keep, full.astype(F32), 0.0).astype(BF16)

    fetch().wait()
    own_piece = (own, 0, clusters)
    hi_a_piece = ((hi_a_0, hi_a_1), clusters, half)
    hi_b_piece = ((hi_b_0, hi_b_1), clusters + half, half)
    lo_a_piece = ((lo_a_0, lo_a_1), -half, half)
    lo_b_piece = ((lo_b_0, lo_b_1), -clusters, half)

    near_phase(0, (own_piece,), 0, clusters, 0)
    wait_halo(0, HI_A)
    near_phase(0, (hi_a_piece,), 0, clusters, 1)
    wait_halo(0, LO_A)
    near_phase(0, (lo_a_piece,), 0, clusters, 1)
    far(0)
    wait_halo(0, HI_B)
    near_phase(0, (hi_b_piece,), half, clusters, 1, (image, first))
    send_halo(1, HI_B)
    send_halo(1, LO_A)
    make_coeffs(1, half, clusters)
    wait_halo(0, LO_B)
    near_phase(0, (lo_b_piece,), 0, half, 1, (image, first))

    send_halo(1, HI_A)
    make_coeffs(1, 0, half)
    send_slots(1)
    send_halo(1, LO_B)
    own_1[:clusters] = image[...]
    near_phase(1, (own_piece,), 0, clusters, 0)
    wait_halo(1, LO_A)
    near_phase(1, (lo_a_piece,), 0, clusters, 1)
    wait_halo(1, HI_B)
    near_phase(1, (hi_b_piece,), half, clusters, 1)
    far(1)
    wait_halo(1, HI_A)
    near_phase(1, (hi_a_piece,), half, clusters, 1, (second,))
    near_phase(1, (hi_a_piece,), 0, half, 1)
    wait_halo(1, LO_B)
    near_phase(1, (lo_b_piece,), 0, half, 1, (second,))

    for sweep in range(2):
        for chunk in range(4):
            halo_sent(sweep, chunk)

        @pl.loop(1, n)
        def _(k):
            slot_copy(sweep, k, lax.rem(me + k, n), me).wait_send()


def on_device(n, input_columns, near_blocks, near_off, basis_in, coupling, basis_out, far_pairs, far_rank):
    clusters, parts, rhs, leaf = input_columns.shape
    near_per = near_blocks.shape[1]
    slots, width = coupling.shape[2], coupling.shape[4]
    rows = parts * rhs
    half = clusters // 2
    vmem = pl.BlockSpec(memory_space=pltpu.VMEM)
    smem = pl.BlockSpec(memory_space=pltpu.SMEM)
    shape = jax.ShapeDtypeStruct((clusters, rows, leaf), BF16)
    halo = pltpu.VMEM((half + 1, rows, leaf), BF16)
    first, second = pl.pallas_call(
        functools.partial(kernel, n),
        out_shape=(shape, shape),
        in_specs=[smem, smem, smem, vmem, pl.BlockSpec(memory_space=pl.ANY), vmem, vmem, vmem],
        out_specs=(vmem, vmem),
        scratch_shapes=[
            pltpu.VMEM(near_blocks.shape, BF16),
            pltpu.VMEM((clusters + 1, rows, leaf), BF16),
            pltpu.VMEM((clusters + 1, rows, leaf), BF16),
            pltpu.VMEM((clusters, rows, leaf), BF16),
            halo, halo, halo, halo,
            halo, halo, halo, halo,
            pltpu.VMEM((clusters, rows, leaf), F32),
            pltpu.VMEM((2, clusters, rhs, 2 * width), BF16),
            pltpu.VMEM((2, n, slots, rhs, 2 * width), BF16),
            pltpu.VMEM((2, n, slots, rhs, 2 * width), BF16),
            pltpu.VMEM((n, slots, 2 * width, 2 * width), BF16),
            pltpu.VMEM((n, slots, rhs, 2 * width), F32),
            pltpu.SemaphoreType.DMA,
            pltpu.SemaphoreType.DMA((2, 4)),
            pltpu.SemaphoreType.DMA((2, 4)),
            pltpu.SemaphoreType.DMA((2, n)),
            pltpu.SemaphoreType.DMA((2, n)),
        ],
        compiler_params=pltpu.CompilerParams(
            collective_id=0, has_side_effects=True, vmem_limit_bytes=60 * 1024 * 1024
        ),
        name="sweeps",
    )(
        near_off.reshape(-1),
        far_pairs.reshape(-1),
        far_rank.reshape(-1),
        input_columns.reshape(clusters, rows, leaf),
        near_blocks,
        basis_in,
        coupling[0],
        basis_out,
    )
    return first.reshape(input_columns.shape), second.reshape(input_columns.shape)


def solution(mesh):
    in_specs = (
        P(("freq", "clus"), None, "rhs", None),
        P(("freq", "clus"), None, None, None, None),
        P("clus", None),
        P(("freq", "clus"), None, None, None),
        P(("freq", "clus"), None, None, None, None, None),
        P(("freq", "clus"), None, None, None),
        P(),
        P(),
    )
    out_specs = (P(("freq", "clus"), None, "rhs", None), P(("freq", "clus"), None, "rhs", None))
    return jax.shard_map(
        functools.partial(on_device, mesh.shape["clus"]),
        mesh=mesh,
        in_specs=in_specs,
        out_specs=out_specs,
        check_vma=False,
    )
```

```python
import functools

import jax
import jax.numpy as jnp
from jax import lax
from jax.experimental import pallas as pl
from jax.experimental.pallas import tpu as pltpu
from jax.sharding import PartitionSpec as P

F32 = jnp.float32
BF16 = jnp.bfloat16

HI_A, HI_B, LO_A, LO_B = range(4)


def complex_rows(product):
    half_rows, half_cols = product.shape[0] // 2, product.shape[1] // 2
    real = product[:half_rows, :half_cols] - product[half_rows:, half_cols:]
    imag = product[:half_rows, half_cols:] + product[half_rows:, :half_cols]
    return real, imag


def kernel(
    n, off, pairs, rank, columns, near_hbm, basis_in_hbm, coupling_hbm, basis_out_hbm,
    first, second,
    near, basis_in, coupling, basis_out, own_0, own_1, hi_a_0, hi_b_0, lo_a_0, lo_b_0, hi_a_1, hi_b_1, lo_a_1, lo_b_1,
    total, coeffs, outgoing, received, square, weighted,
    fetch_sem, halo_send, halo_recv, slot_send, slot_recv,
):
    me = lax.axis_index("clus")
    clusters, rows, leaf = columns.shape
    half = clusters // 2
    slots = coupling.shape[1]
    width = coupling.shape[3]
    near_per = near.shape[1]
    rhs = rows // 2
    own = (own_0, own_1)
    buffers = ((hi_a_0, hi_b_0, lo_a_0, lo_b_0), (hi_a_1, hi_b_1, lo_a_1, lo_b_1))
    fetches = (
        (columns, own_0.at[pl.ds(0, clusters)]),
        (basis_in_hbm, basis_in),
        (near_hbm, near),
        (coupling_hbm, coupling),
        (basis_out_hbm, basis_out),
    )

    def fetch(i):
        return pltpu.make_async_copy(*fetches[i], fetch_sem.at[i])

    barrier = pltpu.get_barrier_semaphore()

    @pl.loop(1, n)
    def _(k):
        pl.semaphore_signal(barrier, inc=1, device_id={"clus": lax.rem(me + k, n)})

    for i in range(len(fetches)):
        fetch(i).start()
    pl.semaphore_wait(barrier, n - 1)

    starts = (0, half, half, 0)

    def halo(sweep, chunk):
        to_left = chunk in (HI_A, HI_B)
        source = columns if sweep == 0 else own_1
        peer = lax.rem(me + (n - 1 if to_left else 1), n)
        return pltpu.make_async_remote_copy(
            src_ref=source.at[pl.ds(starts[chunk], half)],
            dst_ref=buffers[sweep][chunk].at[pl.ds(0, half)],
            send_sem=halo_send.at[sweep, chunk],
            recv_sem=halo_recv.at[sweep, chunk],
            device_id={"clus": peer},
        )

    def send_halo(sweep, chunk):
        @pl.when(me > 0 if chunk in (HI_A, HI_B) else me < n - 1)
        def _():
            halo(sweep, chunk).start()

    def halo_sent(sweep, chunk):
        @pl.when(me > 0 if chunk in (HI_A, HI_B) else me < n - 1)
        def _():
            halo(sweep, chunk).wait_send()

    def wait_halo(sweep, chunk):
        @pl.when(me < n - 1 if chunk in (HI_A, HI_B) else me > 0)
        def _():
            halo(sweep, chunk).wait_recv()

    def slot_copy(sweep, k, peer, sender):
        return pltpu.make_async_remote_copy(
            src_ref=outgoing.at[sweep, peer],
            dst_ref=received.at[sweep, sender],
            send_sem=slot_send.at[sweep, k],
            recv_sem=slot_recv.at[sweep, k],
            device_id={"clus": peer},
        )

    def make_coeffs(sweep, low, high):
        @pl.loop(low, high, unroll=4)
        def _(c):
            v = own[sweep][c]
            basis = basis_in[c].reshape(2 * width, leaf)
            product = lax.dot_general(v, basis, (((1,), (1,)), ((), ())), preferred_element_type=F32)
            real, imag = complex_rows(product)
            coeffs[sweep, c] = jnp.concatenate([real, imag], -1).astype(BF16)

    def send_slots(sweep):
        @pl.loop(1, n)
        def _(k):
            peer = lax.rem(me + k, n)
            for j in range(slots):
                outgoing[sweep, peer, j] = coeffs[sweep, pairs[me, j, 0, peer]]
            slot_copy(sweep, k, peer, me).start()

        for j in range(slots):
            received[sweep, me, j] = coeffs[sweep, pairs[me, j, 0, me]]

    def store(targets, c, real, imag):
        for target in targets:
            target[c, :rhs] = real.astype(target.dtype)
            target[c, rhs:] = imag.astype(target.dtype)

    def near_phase(sweep, piece, low, high, start, finish=None):
        buffers_of, base, count = piece
        buffer = buffers_of[sweep]

        @pl.loop(low, high, unroll=2)
        def _(c):
            product = None
            for j in range(start, near_per, 2):
                left, right = [], []
                for slot in range(j, min(j + 2, near_per)):
                    at = c + off[slot, c] - base
                    at = jnp.where((at >= 0) & (at < count), at, count)
                    left.append(buffer[at])
                    right.append(jnp.concatenate([near[c, slot, 0], near[c, slot, 1]], -1))
                left = left[0] if len(left) == 1 else jnp.concatenate(left, -1)
                right = right[0] if len(right) == 1 else jnp.concatenate(right, 0)
                term = jnp.dot(left, right, preferred_element_type=F32)
                product = term if product is None else product + term
            real, imag = complex_rows(product)
            if start > 0:
                real = total[c, :rhs] + real
                imag = total[c, rhs:] + imag
            store((total,) if finish is None else finish, c, real, imag)

    def far(sweep, finish=None):
        @pl.loop(1, n)
        def _(k):
            sender = lax.rem(me + n - k, n)
            slot_copy(sweep, k, lax.rem(me + k, n), sender).wait_recv()

        @pl.loop(0, n, unroll=2)
        def _(e):
            for j in range(slots):
                weighted[e, j] = jnp.dot(received[sweep, e, j], square[e, j], preferred_element_type=F32)

        def add_far(low, high, targets):
            @pl.loop(low, high, unroll=2)
            def _(c):
                def add(e, value):
                    for j in range(slots):
                        hit = jnp.where(pairs[e, j, 1, me] == c, 1.0, 0.0)
                        value = value + weighted[e, j] * hit
                    return value

                gathered = lax.fori_loop(0, n, add, jnp.zeros((rhs, 2 * width), F32), unroll=4).astype(BF16)
                real, imag = basis_out[c, 0], basis_out[c, 1]
                upper = jnp.concatenate([real, imag], -1)
                lower = jnp.concatenate([-imag, real], -1)
                term = jnp.dot(gathered, jnp.concatenate([upper, lower], 0), preferred_element_type=F32)
                store(targets, c, total[c, :rhs] + term[:, :leaf], total[c, rhs:] + term[:, leaf:])

        add_far(half, clusters, (total,) if finish is None else finish)
        add_far(0, half, (total,))

    send_halo(0, HI_A)
    send_halo(0, LO_A)
    fetch(0).wait()
    fetch(1).wait()
    make_coeffs(0, 0, clusters)
    send_slots(0)
    send_halo(0, HI_B)
    send_halo(0, LO_B)

    zero = jnp.zeros((rows, leaf), BF16)
    for sweep in range(2):
        own[sweep][clusters] = zero
        for buffer in buffers[sweep]:
            buffer[half] = zero

    @pl.when(me == 0)
    def _():
        for sweep in range(2):
            for chunk in (LO_A, LO_B):
                buffers[sweep][chunk][...] = jnp.zeros_like(buffers[sweep][chunk])

    @pl.when(me == n - 1)
    def _():
        for sweep in range(2):
            for chunk in (HI_A, HI_B):
                buffers[sweep][chunk][...] = jnp.zeros_like(buffers[sweep][chunk])

    own_piece = (own, 0, clusters)
    hi_a_piece = ((hi_a_0, hi_a_1), clusters, half)
    hi_b_piece = ((hi_b_0, hi_b_1), clusters + half, half)
    lo_a_piece = ((lo_a_0, lo_a_1), -half, half)
    lo_b_piece = ((lo_b_0, lo_b_1), -clusters, half)

    fetch(2).wait()
    near_phase(0, own_piece, 0, clusters, 0)

    fetch(3).wait()
    fetch(4).wait()

    @pl.loop(0, n)
    def _(e):
        here = lax.broadcasted_iota(jnp.int32, (2 * width, 2 * width), 0) % width
        there = lax.broadcasted_iota(jnp.int32, (2 * width, 2 * width), 1) % width
        position = jnp.maximum(here, there)
        for j in range(slots):
            real, imag = coupling[e, j, 0], coupling[e, j, 1]
            full = jnp.concatenate(
                [jnp.concatenate([real, imag], -1), jnp.concatenate([-imag, real], -1)], 0
            )
            square[e, j] = jnp.where(position < rank[e, j, me], full.astype(F32), 0.0).astype(BF16)

    wait_halo(0, HI_A)
    near_phase(0, hi_a_piece, 0, clusters, 1)
    wait_halo(0, LO_A)
    near_phase(0, lo_a_piece, 0, clusters, 1)
    far(0)
    wait_halo(0, HI_B)
    near_phase(0, hi_b_piece, half, clusters, 1, (own_1, first))
    send_halo(1, HI_B)
    send_halo(1, LO_A)
    make_coeffs(1, half, clusters)
    wait_halo(0, LO_B)
    near_phase(0, lo_b_piece, 0, half, 1, (own_1, first))

    send_halo(1, HI_A)
    make_coeffs(1, 0, half)
    send_slots(1)
    send_halo(1, LO_B)
    near_phase(1, own_piece, 0, clusters, 0)
    wait_halo(1, HI_B)
    near_phase(1, hi_b_piece, half, clusters, 1)
    wait_halo(1, LO_A)
    near_phase(1, lo_a_piece, 0, clusters, 1)
    wait_halo(1, HI_A)
    near_phase(1, hi_a_piece, 0, clusters, 1)
    far(1, (second,))
    wait_halo(1, LO_B)
    near_phase(1, lo_b_piece, 0, half, 1, (second,))

    for sweep in range(2):
        for chunk in range(4):
            halo_sent(sweep, chunk)

        @pl.loop(1, n)
        def _(k):
            slot_copy(sweep, k, lax.rem(me + k, n), me).wait_send()


def on_device(n, input_columns, near_blocks, near_off, basis_in, coupling, basis_out, far_pairs, far_rank):
    clusters, parts, rhs, leaf = input_columns.shape
    near_per = near_blocks.shape[1]
    slots, width = coupling.shape[2], coupling.shape[4]
    rows = parts * rhs
    half = clusters // 2
    vmem = pl.BlockSpec(memory_space=pltpu.VMEM)
    smem = pl.BlockSpec(memory_space=pltpu.SMEM)
    hbm = pl.BlockSpec(memory_space=pltpu.HBM)
    basis_in = jnp.swapaxes(basis_in, 2, 3)
    shape = jax.ShapeDtypeStruct((clusters, rows, leaf), BF16)
    halo = pltpu.VMEM((half + 1, rows, leaf), BF16)
    first, second = pl.pallas_call(
        functools.partial(kernel, n),
        out_shape=(shape, shape),
        in_specs=[smem] * 3 + [hbm] * 5,
        out_specs=(vmem, vmem),
        scratch_shapes=[
            pltpu.VMEM(near_blocks.shape, BF16),
            pltpu.VMEM(basis_in.shape, BF16),
            pltpu.VMEM(coupling.shape[1:], BF16),
            pltpu.VMEM(basis_out.shape, BF16),
            pltpu.VMEM((clusters + 1, rows, leaf), BF16),
            pltpu.VMEM((clusters + 1, rows, leaf), BF16),
            halo, halo, halo, halo,
            halo, halo, halo, halo,
            pltpu.VMEM((clusters, rows, leaf), F32),
            pltpu.VMEM((2, clusters, rhs, 2 * width), BF16),
            pltpu.VMEM((2, n, slots, rhs, 2 * width), BF16),
            pltpu.VMEM((2, n, slots, rhs, 2 * width), BF16),
            pltpu.VMEM((n, slots, 2 * width, 2 * width), BF16),
            pltpu.VMEM((n, slots, rhs, 2 * width), F32),
            pltpu.SemaphoreType.DMA((5,)),
            pltpu.SemaphoreType.DMA((2, 4)),
            pltpu.SemaphoreType.DMA((2, 4)),
            pltpu.SemaphoreType.DMA((2, n)),
            pltpu.SemaphoreType.DMA((2, n)),
        ],
        compiler_params=pltpu.CompilerParams(
            collective_id=0, has_side_effects=True, vmem_limit_bytes=57 * 2**20
        ),
        name="sweeps",
    )(
        near_off.T,
        jnp.transpose(far_pairs, (0, 2, 3, 1)),
        jnp.swapaxes(far_rank, 1, 2),
        input_columns.reshape(clusters, rows, leaf),
        near_blocks,
        basis_in,
        coupling[0],
        basis_out,
    )
    return first.reshape(input_columns.shape), second.reshape(input_columns.shape)


def solution(mesh):
    in_specs = (
        P(("freq", "clus"), None, "rhs", None),
        P(("freq", "clus"), None, None, None, None),
        P("clus", None),
        P(("freq", "clus"), None, None, None),
        P(("freq", "clus"), None, None, None, None, None),
        P(("freq", "clus"), None, None, None),
        P(),
        P(),
    )
    out_specs = (P(("freq", "clus"), None, "rhs", None), P(("freq", "clus"), None, "rhs", None))
    return jax.shard_map(
        functools.partial(on_device, mesh.shape["clus"]),
        mesh=mesh,
        in_specs=in_specs,
        out_specs=out_specs,
        check_vma=False,
    )
```

```python
import functools

import jax
import jax.numpy as jnp
from jax import lax
from jax.experimental import pallas as pl
from jax.experimental.pallas import tpu as pltpu
from jax.sharding import PartitionSpec as P

F32 = jnp.float32
BF16 = jnp.bfloat16

HI_A, HI_B, LO_A, LO_B = range(4)


def complex_rows(product):
    half_rows, half_cols = product.shape[0] // 2, product.shape[1] // 2
    real = product[:half_rows, :half_cols] - product[half_rows:, half_cols:]
    imag = product[:half_rows, half_cols:] + product[half_rows:, :half_cols]
    return real, imag


def kernel(
    n, off, pairs, rank, columns, near_hbm, basis_in_hbm, coupling_hbm, basis_out_hbm,
    first, second,
    near, basis_in, coupling, basis_out, own_0, own_1, hi_a_0, hi_b_0, lo_a_0, lo_b_0, hi_a_1, hi_b_1, lo_a_1, lo_b_1,
    total, coeffs, outgoing, received, square, weighted,
    fetch_sem, halo_send, halo_recv, slot_send, slot_recv,
):
    me = lax.axis_index("clus")
    clusters, rows, leaf = columns.shape
    half = clusters // 2
    slots = coupling.shape[1]
    width = coupling.shape[3]
    near_per = near.shape[1]
    rhs = rows // 2
    own = (own_0, own_1)
    buffers = ((hi_a_0, hi_b_0, lo_a_0, lo_b_0), (hi_a_1, hi_b_1, lo_a_1, lo_b_1))
    fetches = (
        (columns, own_0.at[pl.ds(0, clusters)]),
        (basis_in_hbm, basis_in),
        (near_hbm, near),
        (coupling_hbm, coupling),
        (basis_out_hbm, basis_out),
    )

    def fetch(i):
        return pltpu.make_async_copy(*fetches[i], fetch_sem.at[i])

    barrier = pltpu.get_barrier_semaphore()

    @pl.loop(1, n)
    def _(k):
        pl.semaphore_signal(barrier, inc=1, device_id={"clus": lax.rem(me + k, n)})

    for i in range(len(fetches)):
        fetch(i).start()
    pl.semaphore_wait(barrier, n - 1)

    starts = (0, half, half, 0)

    def halo(sweep, chunk):
        to_left = chunk in (HI_A, HI_B)
        source = columns if sweep == 0 else own_1
        peer = lax.rem(me + (n - 1 if to_left else 1), n)
        return pltpu.make_async_remote_copy(
            src_ref=source.at[pl.ds(starts[chunk], half)],
            dst_ref=buffers[sweep][chunk].at[pl.ds(0, half)],
            send_sem=halo_send.at[sweep, chunk],
            recv_sem=halo_recv.at[sweep, chunk],
            device_id={"clus": peer},
        )

    def send_halo(sweep, chunk):
        @pl.when(me > 0 if chunk in (HI_A, HI_B) else me < n - 1)
        def _():
            halo(sweep, chunk).start()

    def halo_sent(sweep, chunk):
        @pl.when(me > 0 if chunk in (HI_A, HI_B) else me < n - 1)
        def _():
            halo(sweep, chunk).wait_send()

    def wait_halo(sweep, chunk):
        @pl.when(me < n - 1 if chunk in (HI_A, HI_B) else me > 0)
        def _():
            halo(sweep, chunk).wait_recv()

    def slot_copy(sweep, k, peer, sender):
        return pltpu.make_async_remote_copy(
            src_ref=outgoing.at[sweep, peer],
            dst_ref=received.at[sweep, sender],
            send_sem=slot_send.at[sweep, k],
            recv_sem=slot_recv.at[sweep, k],
            device_id={"clus": peer},
        )

    def make_coeffs(sweep, low, high):
        @pl.loop(low, high, unroll=4)
        def _(c):
            v = own[sweep][c]
            basis = basis_in[c].reshape(2 * width, leaf)
            product = lax.dot_general(v, basis, (((1,), (1,)), ((), ())), preferred_element_type=F32)
            real, imag = complex_rows(product)
            coeffs[sweep, c] = jnp.concatenate([real, imag], -1).astype(BF16)

    def send_slots(sweep, part, of):
        @pl.loop(1 + (n - 1) * part // of, 1 + (n - 1) * (part + 1) // of)
        def _(k):
            peer = lax.rem(me + k, n)
            for j in range(slots):
                outgoing[sweep, peer, j] = coeffs[sweep, pairs[me, j, 0, peer]]
            slot_copy(sweep, k, peer, me).start()

        for j in range(slots if part == 0 else 0):
            received[sweep, me, j] = coeffs[sweep, pairs[me, j, 0, me]]

    def store(targets, c, real, imag):
        for target in targets:
            target[c, :rhs] = real.astype(target.dtype)
            target[c, rhs:] = imag.astype(target.dtype)

    def near_phase(sweep, piece, low, high, start, finish=None):
        buffers_of, base, count = piece
        buffer = buffers_of[sweep]

        @pl.loop(low, high, unroll=2)
        def _(c):
            product = None
            for j in range(start, near_per, 2):
                left, right = [], []
                for slot in range(j, min(j + 2, near_per)):
                    at = c + off[slot, c] - base
                    at = jnp.where((at >= 0) & (at < count), at, count)
                    left.append(buffer[at])
                    right.append(jnp.concatenate([near[c, slot, 0], near[c, slot, 1]], -1))
                left = left[0] if len(left) == 1 else jnp.concatenate(left, -1)
                right = right[0] if len(right) == 1 else jnp.concatenate(right, 0)
                term = jnp.dot(left, right, preferred_element_type=F32)
                product = term if product is None else product + term
            real, imag = complex_rows(product)
            if start > 0:
                real = total[c, :rhs] + real
                imag = total[c, rhs:] + imag
            store((total,) if finish is None else finish, c, real, imag)

    def far(sweep, finish=None):
        @pl.loop(1, n)
        def _(k):
            sender = lax.rem(me + n - k, n)
            slot_copy(sweep, k, lax.rem(me + k, n), sender).wait_recv()

        @pl.loop(0, n, unroll=2)
        def _(e):
            for j in range(slots):
                weighted[e, j] = jnp.dot(received[sweep, e, j], square[e, j], preferred_element_type=F32)

        def add_far(low, high, targets):
            @pl.loop(low, high, unroll=2)
            def _(c):
                def add(e, value):
                    for j in range(slots):
                        hit = jnp.where(pairs[e, j, 1, me] == c, 1.0, 0.0)
                        value = value + weighted[e, j] * hit
                    return value

                gathered = lax.fori_loop(0, n, add, jnp.zeros((rhs, 2 * width), F32), unroll=4).astype(BF16)
                real, imag = basis_out[c, 0], basis_out[c, 1]
                upper = jnp.concatenate([real, imag], -1)
                lower = jnp.concatenate([-imag, real], -1)
                term = jnp.dot(gathered, jnp.concatenate([upper, lower], 0), preferred_element_type=F32)
                store(targets, c, total[c, :rhs] + term[:, :leaf], total[c, rhs:] + term[:, leaf:])

        add_far(half, clusters, (total,) if finish is None else finish)
        add_far(0, half, (total,))

    fetch(0).wait()
    fetch(1).wait()
    make_coeffs(0, 0, clusters)
    send_slots(0, 0, 1)
    send_halo(0, HI_A)
    send_halo(0, LO_A)
    send_halo(0, HI_B)
    send_halo(0, LO_B)

    zero = jnp.zeros((rows, leaf), BF16)
    for sweep in range(2):
        own[sweep][clusters] = zero
        for buffer in buffers[sweep]:
            buffer[half] = zero

    @pl.when(me == 0)
    def _():
        for sweep in range(2):
            for chunk in (LO_A, LO_B):
                buffers[sweep][chunk][...] = jnp.zeros_like(buffers[sweep][chunk])

    @pl.when(me == n - 1)
    def _():
        for sweep in range(2):
            for chunk in (HI_A, HI_B):
                buffers[sweep][chunk][...] = jnp.zeros_like(buffers[sweep][chunk])

    own_piece = (own, 0, clusters)
    hi_a_piece = ((hi_a_0, hi_a_1), clusters, half)
    hi_b_piece = ((hi_b_0, hi_b_1), clusters + half, half)
    lo_a_piece = ((lo_a_0, lo_a_1), -half, half)
    lo_b_piece = ((lo_b_0, lo_b_1), -clusters, half)

    fetch(2).wait()
    near_phase(0, own_piece, 0, clusters, 0)

    fetch(3).wait()
    fetch(4).wait()

    @pl.loop(0, n)
    def _(e):
        here = lax.broadcasted_iota(jnp.int32, (2 * width, 2 * width), 0) % width
        there = lax.broadcasted_iota(jnp.int32, (2 * width, 2 * width), 1) % width
        position = jnp.maximum(here, there)
        for j in range(slots):
            real, imag = coupling[e, j, 0], coupling[e, j, 1]
            full = jnp.concatenate(
                [jnp.concatenate([real, imag], -1), jnp.concatenate([-imag, real], -1)], 0
            )
            square[e, j] = jnp.where(position < rank[e, j, me], full.astype(F32), 0.0).astype(BF16)

    wait_halo(0, HI_A)
    near_phase(0, hi_a_piece, 0, clusters, 1)
    wait_halo(0, LO_A)
    near_phase(0, lo_a_piece, 0, clusters, 1)
    far(0)
    wait_halo(0, HI_B)
    near_phase(0, hi_b_piece, half, clusters, 1, (own_1, first))
    send_halo(1, HI_B)
    send_halo(1, LO_A)
    make_coeffs(1, half, clusters)
    wait_halo(0, LO_B)
    near_phase(0, lo_b_piece, 0, half, 1, (own_1, first))

    make_coeffs(1, 0, half)
    send_slots(1, 0, 1)
    send_halo(1, HI_A)
    send_halo(1, LO_B)
    near_phase(1, own_piece, 0, clusters, 0)
    wait_halo(1, HI_B)
    near_phase(1, hi_b_piece, half, clusters, 1)
    wait_halo(1, LO_A)
    near_phase(1, lo_a_piece, 0, clusters, 1)
    wait_halo(1, HI_A)
    near_phase(1, hi_a_piece, 0, clusters, 1)
    far(1, (second,))
    wait_halo(1, LO_B)
    near_phase(1, lo_b_piece, 0, half, 1, (second,))

    for sweep in range(2):
        for chunk in range(4):
            halo_sent(sweep, chunk)

        @pl.loop(1, n)
        def _(k):
            slot_copy(sweep, k, lax.rem(me + k, n), me).wait_send()


def on_device(n, input_columns, near_blocks, near_off, basis_in, coupling, basis_out, far_pairs, far_rank):
    clusters, parts, rhs, leaf = input_columns.shape
    near_per = near_blocks.shape[1]
    slots, width = coupling.shape[2], coupling.shape[4]
    rows = parts * rhs
    half = clusters // 2
    vmem = pl.BlockSpec(memory_space=pltpu.VMEM)
    smem = pl.BlockSpec(memory_space=pltpu.SMEM)
    hbm = pl.BlockSpec(memory_space=pltpu.HBM)
    basis_in = jnp.swapaxes(basis_in, 2, 3)
    shape = jax.ShapeDtypeStruct((clusters, rows, leaf), BF16)
    halo = pltpu.VMEM((half + 1, rows, leaf), BF16)
    first, second = pl.pallas_call(
        functools.partial(kernel, n),
        out_shape=(shape, shape),
        in_specs=[smem] * 3 + [hbm] * 5,
        out_specs=(vmem, vmem),
        scratch_shapes=[
            pltpu.VMEM(near_blocks.shape, BF16),
            pltpu.VMEM(basis_in.shape, BF16),
            pltpu.VMEM(coupling.shape[1:], BF16),
            pltpu.VMEM(basis_out.shape, BF16),
            pltpu.VMEM((clusters + 1, rows, leaf), BF16),
            pltpu.VMEM((clusters + 1, rows, leaf), BF16),
            halo, halo, halo, halo,
            halo, halo, halo, halo,
            pltpu.VMEM((clusters, rows, leaf), F32),
            pltpu.VMEM((2, clusters, rhs, 2 * width), BF16),
            pltpu.VMEM((2, n, slots, rhs, 2 * width), BF16),
            pltpu.VMEM((2, n, slots, rhs, 2 * width), BF16),
            pltpu.VMEM((n, slots, 2 * width, 2 * width), BF16),
            pltpu.VMEM((n, slots, rhs, 2 * width), F32),
            pltpu.SemaphoreType.DMA((5,)),
            pltpu.SemaphoreType.DMA((2, 4)),
            pltpu.SemaphoreType.DMA((2, 4)),
            pltpu.SemaphoreType.DMA((2, n)),
            pltpu.SemaphoreType.DMA((2, n)),
        ],
        compiler_params=pltpu.CompilerParams(
            collective_id=0, has_side_effects=True, vmem_limit_bytes=52 * 2**20
        ),
        name="sweeps",
    )(
        near_off.T,
        jnp.transpose(far_pairs, (0, 2, 3, 1)),
        jnp.swapaxes(far_rank, 1, 2),
        input_columns.reshape(clusters, rows, leaf),
        near_blocks,
        basis_in,
        coupling[0],
        basis_out,
    )
    return first.reshape(input_columns.shape), second.reshape(input_columns.shape)


def solution(mesh):
    in_specs = (
        P(("freq", "clus"), None, "rhs", None),
        P(("freq", "clus"), None, None, None, None),
        P("clus", None),
        P(("freq", "clus"), None, None, None),
        P(("freq", "clus"), None, None, None, None, None),
        P(("freq", "clus"), None, None, None),
        P(),
        P(),
    )
    out_specs = (P(("freq", "clus"), None, "rhs", None), P(("freq", "clus"), None, "rhs", None))
    return jax.shard_map(
        functools.partial(on_device, mesh.shape["clus"]),
        mesh=mesh,
        in_specs=in_specs,
        out_specs=out_specs,
        check_vma=False,
    )
```
